32 devices in a mesh: ent: 16 (over z, y, x), rep: 2 (over core).
Axes of the slice: x: 2, y: 2, z: 4, core: 2. Of those that a mesh axis runs over, the one named last changes fastest.
Arguments:
- head_ids: int32 [8192], P(('ent', 'rep')), may hold values from 0 to 32767, as said below
- rel_ids: int32 [8192], P(('ent', 'rep')), may hold values from 0 to 4095
- tail_ids: int32 [8192], P(('ent', 'rep')), may hold values from 0 to 32767, as said below
- neg_ids: int32 [256], P('ent'), may hold values from 0 to 32767, as said below
- slot_of: int32 [32768], replicated, may hold values from 0 to 32767, as said below
- relations: bfloat16 [4096, 400], replicated, may hold values from -3 to 3
- embeddings: float32 [32768, 400], P('ent'), may hold values from -1.75 to 1.75
- accumulator: float32 [32768], P('ent'), may hold values from 0.001 to 0.03
Outputs:
- new_embeddings: float32 [32768, 400], P('ent')
- new_accumulator: float32 [32768], P('ent')
The draws below stay inside these ranges and needn't reach their ends.
Inputs may be any that keep to these rules, and one draw needn't show every extreme that they name: A permutation: every table row stores exactly one entity; the owner of entity e is slot_of[e] // 2048. `head_ids`: among the 512 endpoints (heads and tails together) of the edges of one device, at most 64 have any one owner; in every draw one owner has exactly 64 endpoints of every device. `tail_ids`: see head_ids: the bound counts heads and tails of one device together. `neg_ids`: entry j has owner j // 16.
All inputs are finite; a program needn't handle non-finite values.
Results may differ from the reference program's by a relative error of at most 0.0031.
Values may be sent and summed in bfloat16 or wider, within the bound.
No kernel may reach another device: no remote copies, remote signals or barrier semaphores. Data moves between devices by JAX's collectives and lax.ppermute only.
A program may use at most 128 MiB of HBM per device.

```python
import math
import jax
import jax.numpy as jnp
from jax import lax

D = 400
REL = 4096
E_DEV = 2048
EDGE_DEV = 256
NEG_DEV = 16
OWNERS = 16
WORKERS = 32
NE = 32768
EDGES = 8192
CAP = 64
NEG = 256


def entity_order(key):
    return jax.random.permutation(jax.random.fold_in(key, 11), NE).astype(jnp.int32)


def endpoint_ids(key):
    ent_of_slot = entity_order(key)
    hot_owner = jax.random.randint(jax.random.fold_in(key, 12), (), 0, OWNERS)
    end_count = 2 * EDGE_DEV

    def one_block(block_index):
        block_key = jax.random.fold_in(jax.random.fold_in(key, 13), block_index)
        pool = jax.random.permutation(jax.random.fold_in(block_key, 1), (OWNERS - 1) * CAP)[:end_count - CAP] // CAP
        others = (hot_owner + 1 + pool) % OWNERS
        owner_list = jnp.concatenate([jnp.full((CAP,), hot_owner, jnp.int32), others.astype(jnp.int32)])
        owner_list = jax.random.permutation(jax.random.fold_in(block_key, 2), owner_list)
        row_pick = jax.random.randint(jax.random.fold_in(block_key, 3), (end_count,), 0, E_DEV)
        return ent_of_slot[owner_list * E_DEV + row_pick]
    return jax.vmap(one_block)(jnp.arange(WORKERS))


def draw_head_ids(key, part):
    return endpoint_ids(key)[:, :EDGE_DEV].reshape(-1).astype(jnp.int32)


def draw_tail_ids(key, part):
    return endpoint_ids(key)[:, EDGE_DEV:].reshape(-1).astype(jnp.int32)


def draw_slot_of(key, part):
    return jnp.argsort(entity_order(key), stable=True).astype(jnp.int32)


def draw_neg_ids(key, part):
    ent_of_slot = entity_order(key)
    row_pick = jax.random.randint(jax.random.fold_in(key, 14), (NEG,), 0, E_DEV)
    owner_list = jnp.arange(NEG, dtype=jnp.int32) // NEG_DEV
    return ent_of_slot[owner_list * E_DEV + row_pick].astype(jnp.int32)


def plant(entries, rng, low, top_value):
    spot = [jax.random.randint(jax.random.fold_in(rng, axis), (), 0, length) for axis, length in enumerate(entries.shape)]
    widest = entries.shape.index(max(entries.shape))
    next_to = spot[:widest] + [(spot[widest] + 1) % entries.shape[widest]] + spot[widest + 1:]
    return entries.at[tuple(spot)].set(low).at[tuple(next_to)].set(top_value)


def steps_of(key, dims, split, least, top_value):
    loudness, own = 1.0, jax.random.fold_in(key, 6)
    for axis_at, blocks in split:
        steps = jnp.exp(jax.random.uniform(jax.random.fold_in(own, axis_at), (blocks,), jnp.float32, least / len(split), top_value / len(split)))
        loudness = loudness * jnp.repeat(steps, dims[axis_at] // blocks).reshape([-1 if axis == axis_at else 1 for axis in range(len(dims))])
    return loudness


def centred(own_key, dims, scale, reach, pieces=(), held_as=jnp.bfloat16):
    factor_of = steps_of(own_key, dims, pieces, -0.22, 0.18) if pieces else 1.0
    array = jax.random.normal(own_key, dims, jnp.float32) * scale * factor_of
    return jnp.minimum(jnp.maximum(array, -reach), reach).astype(held_as)


def setup_inputs(seed: int = 0) -> dict:
    key_of = jax.random.split(jax.random.key(seed), 9)
    head_ids = draw_head_ids(jax.random.fold_in(key_of[8], 71), 0)
    rel_ids = plant(jax.random.randint(key_of[1], (EDGES,), 0, REL), jax.random.fold_in(key_of[1], 1), 0, REL - 1).astype(jnp.int32)
    tail_ids = draw_tail_ids(jax.random.fold_in(key_of[8], 71), 0)
    neg_ids = draw_neg_ids(jax.random.fold_in(key_of[8], 71), 0)
    slot_of = draw_slot_of(jax.random.fold_in(key_of[8], 71), 0)
    relations = centred(key_of[5], (REL, D), 0.5, 3.0)
    embeddings = centred(key_of[6], (NE, D), 0.3, 1.75, ((0, 16),), jnp.float32)
    accumulator = jnp.clip(jnp.exp(math.log(0.03) - 3.4011973 * jax.random.uniform(key_of[7], (NE,), jnp.float32) ** steps_of(key_of[7], (NE,), ((0, 16),), -0.2, 0.2)), 0.001, 0.03)
    return dict(head_ids=head_ids, rel_ids=rel_ids, tail_ids=tail_ids, neg_ids=neg_ids, slot_of=slot_of, relations=relations, embeddings=embeddings, accumulator=accumulator)


step_rate = 0.3

def split_parts(values):
    cut = values.shape[1] // 2
    return (values[:, :cut], values[:, cut:])

def edge_terms(head_rows, rel_rows, tail_rows, neg_rows):
    head_full = head_rows.astype(jnp.float32)
    rel_full = rel_rows.astype(jnp.float32)
    tail_full = tail_rows.astype(jnp.float32)
    head_re, head_im = split_parts(head_full)
    rel_re, rel_im = split_parts(rel_full)
    tail_re, tail_im = split_parts(tail_full)
    product = jnp.concatenate([head_re * rel_re - head_im * rel_im, head_re * rel_im + head_im * rel_re], axis=1)
    product_low = product.astype(jnp.bfloat16)
    mirror_low = jnp.concatenate([rel_re * tail_re + rel_im * tail_im, rel_re * tail_im - rel_im * tail_re], axis=1).astype(jnp.bfloat16)
    positive = lax.optimization_barrier(jnp.sum(product * tail_full, axis=1))
    inner_dims = (((1,), (1,)), ((), ()))
    tail_scores = lax.dot_general(product_low, neg_rows, inner_dims, preferred_element_type=jnp.float32)
    head_scores = lax.dot_general(mirror_low, neg_rows, inner_dims, preferred_element_type=jnp.float32)
    neg_count = neg_rows.shape[0]
    pos_grad = -jax.nn.sigmoid(-positive)
    tail_weight = (jax.nn.sigmoid(tail_scores) / neg_count).astype(jnp.bfloat16)
    head_weight = (jax.nn.sigmoid(head_scores) / neg_count).astype(jnp.bfloat16)
    product_grad = jnp.dot(tail_weight, neg_rows, preferred_element_type=jnp.float32) + pos_grad[:, None] * tail_full
    mirror_grad = jnp.dot(head_weight, neg_rows, preferred_element_type=jnp.float32)
    edge_dims = (((0,), (0,)), ((), ()))
    neg_grad = lax.dot_general(tail_weight, product_low, edge_dims, preferred_element_type=jnp.float32)
    neg_grad = neg_grad + lax.dot_general(head_weight, mirror_low, edge_dims, preferred_element_type=jnp.float32)
    grad_re, grad_im = split_parts(product_grad)
    head_grad = jnp.concatenate([grad_re * rel_re + grad_im * rel_im, grad_im * rel_re - grad_re * rel_im], axis=1)
    back_re, back_im = split_parts(mirror_grad)
    tail_grad = pos_grad[:, None] * product + jnp.concatenate([back_re * rel_re - back_im * rel_im, back_re * rel_im + back_im * rel_re], axis=1)
    return (head_grad, tail_grad, neg_grad)

def row_update(old_rows, old_state, gradient):
    new_state = old_state + lax.optimization_barrier(jnp.mean(gradient * gradient, axis=1))
    new_rows = old_rows - step_rate * gradient / jnp.sqrt(new_state)[:, None]
    return (new_rows, new_state)

def reference(head_ids, rel_ids, tail_ids, neg_ids, slot_of, relations, embeddings, accumulator):
    feature_count = embeddings.shape[1]
    low_table = embeddings.astype(jnp.bfloat16)
    neg_rows = low_table[slot_of[neg_ids]]

    def block_step(running, edge_block):
        head_block, rel_block, tail_block = edge_block
        head_part, tail_part, neg_part = edge_terms(low_table[slot_of[head_block]], relations[rel_block], low_table[slot_of[tail_block]], neg_rows)
        return (running + neg_part, (head_part, tail_part))
    blocks = (head_ids.reshape(-1, EDGE_DEV), rel_ids.reshape(-1, EDGE_DEV), tail_ids.reshape(-1, EDGE_DEV))
    neg_total, (head_grads, tail_grads) = lax.scan(block_step, jnp.zeros((NEG, feature_count), jnp.float32), blocks)
    gradient = jnp.zeros(embeddings.shape, jnp.float32)
    gradient = gradient.at[slot_of[head_ids]].add(head_grads.reshape(-1, feature_count))
    gradient = gradient.at[slot_of[tail_ids]].add(tail_grads.reshape(-1, feature_count))
    gradient = gradient.at[slot_of[neg_ids]].add(neg_total)
    new_rows, new_state = row_update(embeddings, accumulator, gradient)
    return (new_rows, new_state)
```

```python
import functools

import jax
import jax.numpy as jnp
from jax import lax
from jax.experimental import pallas as pl
from jax.experimental.pallas import tpu as pltpu
from jax.sharding import PartitionSpec as P

step_rate = 0.3
bf16 = jnp.bfloat16
f32 = jnp.float32
i32 = jnp.int32
LANES = 128
VMEM = pl.BlockSpec(memory_space=pltpu.VMEM)
SMEM = pl.BlockSpec(memory_space=pltpu.SMEM)
ANY = pl.BlockSpec(memory_space=pl.ANY)
NN = (((1,), (0,)), ((), ()))
NT = (((1,), (1,)), ((), ()))
TN = (((0,), (0,)), ((), ()))


def mm(a, b, dims=NN):
    return lax.dot_general(a, b, dims, preferred_element_type=f32)


def iota(shape, axis):
    return lax.broadcasted_iota(i32, shape, axis)


def onehot(flags):
    return flags.astype(f32).astype(bf16)


def halves_swapped(values):
    return pltpu.roll(values, LANES // 2, 1)


def request_kernel(
    row_count, owner_count, capacity, neg_own,
    head_ref, tail_ref, neg_ref, slot_ref, emb_ref,
    pay_ref, place_ref, neg_row_ref, table_ref,
    emb_buf, neg_buf, sems,
):
    feature_count = emb_ref.shape[0]
    chunk = feature_count // 2
    copies = [
        pltpu.make_async_copy(
            emb_ref.at[pl.ds(c * chunk, chunk)], emb_buf.at[pl.ds(c * chunk, chunk)], sems.at[c]
        )
        for c in range(2)
    ]
    for copy in copies:
        copy.start()
    slots = slot_ref[...]
    slots_low = (slots & 255).astype(f32).astype(bf16)
    slots_high = (slots >> 8).astype(f32).astype(bf16)

    def lookup(ids):
        count = ids.shape[1]
        picks = onehot(iota((slots.shape[0], count), 0) == (ids >> 7))
        columns = mm(slots_low, picks, TN) + 256.0 * mm(slots_high, picks, TN)
        lane_of = iota((LANES, count), 0) == (ids & 127)
        return jnp.sum(jnp.where(lane_of, columns, 0.0), axis=0, keepdims=True).astype(i32)

    ids = jnp.concatenate([head_ref[...], tail_ref[...]], axis=1)
    end_count = ids.shape[1]
    end_slots = lookup(ids)
    owner_of = end_slots // row_count
    local_row = end_slots - owner_of * row_count + 1
    owners = iota((owner_count, end_count), 0) == owner_of
    earlier = onehot(iota((end_count, end_count), 0) < iota((end_count, end_count), 1))
    before = mm(onehot(owners), earlier)
    rank = jnp.sum(jnp.where(owners, before, 0.0), axis=0, keepdims=True).astype(i32)
    place_ref[...] = owner_of * capacity + rank
    low = jnp.where(owners, (local_row & 255).astype(f32), 0.0).astype(bf16)
    high = jnp.where(owners, (local_row >> 8).astype(f32), 0.0).astype(bf16)
    lane = iota((LANES, end_count), 0)
    requests = mm(low, onehot(lane == rank), NT) + mm(high, onehot(lane == rank + capacity), NT)

    lane_row = iota((1, LANES), 1)
    neg_ids = jnp.zeros((1, LANES), i32)
    for n in range(neg_own):
        neg_ids = jnp.where(lane_row % neg_own == n, neg_ref[n], neg_ids)
    neg_row = lookup(neg_ids)
    neg_row = neg_row - (neg_row // row_count) * row_count
    neg_row_ref[...] = neg_row
    for copy in copies:
        copy.wait()
    table_ref[...] = emb_buf[...].astype(bf16)
    neg_buf[...] = mm(table_ref[...], onehot(iota((row_count, LANES), 0) == neg_row))
    groups = LANES // neg_own
    piece = feature_count // groups
    packed = jnp.zeros((piece, LANES), f32)
    for g in range(groups):
        packed = jnp.where(lane_row // neg_own == g, neg_buf[pl.ds(g * piece, piece), :], packed)
    neg_buf[pl.ds(0, piece), :] = packed
    neg_buf[pl.ds(piece, 8), :] = jnp.zeros((8, LANES), f32)
    whole = piece // 16 * 16
    main = neg_buf[pl.ds(0, whole), :].astype(bf16)
    rest_rows = pay_ref.shape[1] - whole
    rest = neg_buf[pl.ds(whole, rest_rows), :]
    is_request = iota((rest_rows, LANES), 0) == piece - whole
    for d in range(owner_count):
        pay_ref[d, 0:whole, :] = main
        pay_ref[d, whole : whole + rest_rows, :] = jnp.where(
            is_request, requests[d : d + 1, :], rest
        ).astype(bf16)


def asked_lanes(req, owner_count):
    value = req + 256.0 * halves_swapped(req)
    other = halves_swapped(value)
    left = iota((1, LANES), 1) < LANES // 2
    rows = [
        jnp.where(left, value[s : s + 1, :], other[s + 1 : s + 2, :])
        for s in range(0, owner_count, 2)
    ]
    return jnp.concatenate(rows, axis=1).astype(i32)


def pack_pair(values):
    half = values.shape[0] // 2
    real, imag = values[:half], values[half:]
    left = iota((half, LANES), 1) < LANES // 2
    first = jnp.where(left, real, halves_swapped(imag))
    second = jnp.where(left, halves_swapped(real), imag)
    return first.astype(bf16), second.astype(bf16)


def unpack_pair(first, second):
    first, second = first.astype(f32), second.astype(f32)
    left = iota(first.shape, 1) < LANES // 2
    real = jnp.where(left, first, halves_swapped(second))
    imag = jnp.where(left, halves_swapped(first), second)
    return real.astype(bf16), imag.astype(bf16)


def answer_kernel(owner_count, req_row, got_ref, table_ref, out_ref, asked_ref):
    row_count = table_ref.shape[1]
    asked = asked_lanes(got_ref[:, req_row, :].astype(f32), owner_count)
    asked_ref[...] = asked
    width = 2 * LANES
    for c in range(asked.shape[1] // width):
        row = asked[:, c * width : (c + 1) * width]
        picks = onehot(iota((row_count, width), 0) + 1 == row)
        rows = mm(table_ref[...], picks)
        for p in range(2):
            first, second = pack_pair(rows[:, p * LANES : (p + 1) * LANES])
            out_ref[4 * c + 2 * p] = first
            out_ref[4 * c + 2 * p + 1] = second


def relation_kernel(ids_ref, relations_ref, out_ref):
    count = relations_ref.shape[1]
    picks = onehot(iota((count, ids_ref.shape[1]), 0) == ids_ref[...])
    out_ref[...] = mm(relations_ref[...], picks).astype(bf16)


def edge_kernel(owner_count, got_ref, rel_ref, neg_ref, place_ref, out_ref, rows_buf):
    half = got_ref.shape[1]
    slot_count = rows_buf.shape[1]
    end_count = place_ref.shape[1]
    edge_count = end_count // 2
    for s in range(0, owner_count, 2):
        real, imag = unpack_pair(got_ref[s], got_ref[s + 1])
        lanes = pl.ds(s // 2 * LANES, LANES)
        rows_buf[0:half, lanes] = real.astype(f32)
        rows_buf[half : 2 * half, lanes] = imag.astype(f32)
    places = onehot(iota((slot_count, end_count), 0) == place_ref[...])
    ends = mm(rows_buf[...].astype(bf16), places)
    head_re, head_im = ends[:half, :edge_count], ends[half:, :edge_count]
    tail_re, tail_im = ends[:half, edge_count:], ends[half:, edge_count:]
    rel = rel_ref[...].astype(f32)
    rel_re, rel_im = rel[:half], rel[half:]
    neg = neg_ref[...]
    neg_count = neg.shape[0]
    product_re = head_re * rel_re - head_im * rel_im
    product_im = head_re * rel_im + head_im * rel_re
    product_low = jnp.concatenate([product_re, product_im], axis=0).astype(bf16)
    mirror_low = jnp.concatenate(
        [rel_re * tail_re + rel_im * tail_im, rel_re * tail_im - rel_im * tail_re], axis=0
    ).astype(bf16)
    positive = jnp.sum(product_re * tail_re + product_im * tail_im, axis=0, keepdims=True)
    pos_grad = -jax.nn.sigmoid(-positive)
    tail_weight = (jax.nn.sigmoid(mm(neg, product_low)) / neg_count).astype(bf16)
    head_weight = (jax.nn.sigmoid(mm(neg, mirror_low)) / neg_count).astype(bf16)
    neg_grad = mm(tail_weight, product_low, NT) + mm(head_weight, mirror_low, NT)
    own = neg_count // owner_count
    tiles = (2 * half + LANES - 1) // LANES
    neg_low = neg_grad.astype(bf16)
    for t in range(tiles):
        width = min(LANES, 2 * half - t * LANES)
        for d in range(owner_count):
            out_ref[d, t * own : (t + 1) * own, 0:width] = neg_low[
                d * own : (d + 1) * own, t * LANES : t * LANES + width
            ]
    grad = mm(neg, tail_weight, TN)
    back = mm(neg, head_weight, TN)
    grad_re = grad[:half] + pos_grad * tail_re
    grad_im = grad[half:] + pos_grad * tail_im
    back_re, back_im = back[:half], back[half:]
    head_grad = jnp.concatenate(
        [grad_re * rel_re + grad_im * rel_im, grad_im * rel_re - grad_re * rel_im], axis=0
    ).astype(bf16)
    tail_grad = jnp.concatenate(
        [
            pos_grad * product_re + (back_re * rel_re - back_im * rel_im),
            pos_grad * product_im + (back_re * rel_im + back_im * rel_re),
        ],
        axis=0,
    ).astype(bf16)
    grads = jnp.concatenate([head_grad, tail_grad], axis=1)
    base = tiles * own
    width = 2 * LANES
    for c in range(slot_count // width):
        sent = mm(grads, places[c * width : (c + 1) * width, :], NT)
        for p in range(2):
            first, second = pack_pair(sent[:, p * LANES : (p + 1) * LANES])
            out_ref[4 * c + 2 * p, base : base + half, :] = first
            out_ref[4 * c + 2 * p + 1, base : base + half, :] = second


def gather_grads(owner_count, base, got_ref, buf):
    half = got_ref.shape[1] - base
    own = base // 4
    slot_count = owner_count * LANES // 2
    for s in range(0, owner_count, 2):
        real, imag = unpack_pair(got_ref[s, base:, :], got_ref[s + 1, base:, :])
        lanes = pl.ds(s // 2 * LANES, LANES)
        buf[0:half, lanes] = real
        buf[half : 2 * half, lanes] = imag
    total = got_ref[0, 0:base, :].astype(f32)
    for s in range(1, owner_count):
        total = total + got_ref[s, 0:base, :].astype(f32)
    parts = [total[t * own : (t + 1) * own].T for t in range(4)]
    neg = jnp.concatenate(parts, axis=0)[: 2 * half]
    high = neg.astype(bf16)
    buf[0 : 2 * half, slot_count : slot_count + own] = high
    buf[0 : 2 * half, slot_count + own : slot_count + 2 * own] = (neg - high.astype(f32)).astype(bf16)


def sum_kernel(owner_count, base, own, got_ref, asked_ref, neg_row_ref, out_ref, buf):
    @pl.when(pl.program_id(0) == 0)
    def _():
        gather_grads(owner_count, base, got_ref, buf)

    out_ref[...] = block_sum(own, asked_ref, neg_row_ref, buf, out_ref.shape[1])


def block_sum(own, asked_ref, neg_row_ref, buf, rows):
    first = pl.program_id(0) * rows
    asked = jnp.concatenate([asked_ref[...], neg_row_ref[:, 0 : 2 * own] + 1], axis=1)
    targets = onehot(iota((rows, asked.shape[1]), 0) + first + 1 == asked)
    return mm(buf[...], targets, NT)


def update_kernel(
    owner_count, base, own,
    got_ref, asked_ref, neg_row_ref, mine_ref, emb_ref, acc_ref, new_ref, state_ref, buf,
):
    @pl.when(pl.program_id(0) == 0)
    def _():
        gather_grads(owner_count, base, got_ref, buf)

    grad = mine_ref[...] + block_sum(own, asked_ref, neg_row_ref, buf, new_ref.shape[1])
    state = acc_ref[...] + jnp.sum(grad * grad, axis=0, keepdims=True) / grad.shape[0]
    state_ref[...] = state
    new_ref[...] = emb_ref[...] - grad * (step_rate / jnp.sqrt(state))


def call(kernel, outs, in_specs, scratch=(), limit=40 << 20, cost=None, **grid):
    return pl.pallas_call(
        kernel,
        out_shape=outs,
        in_specs=in_specs,
        scratch_shapes=list(scratch),
        compiler_params=pltpu.CompilerParams(vmem_limit_bytes=limit),
        cost_estimate=cost,
        **grid,
    )


def cost(flops, moved):
    return pl.CostEstimate(flops=flops, bytes_accessed=moved, transcendentals=0)


def exchange(values):
    return lax.all_to_all(values, "ent", split_axis=0, concat_axis=0, tiled=True)


def packed_shards(
    head_ids, rel_ids, tail_ids, neg_ids, slot_of, relations, embeddings, accumulator
):
    row_count, features = embeddings.shape
    half = features // 2
    owners = lax.axis_size("ent")
    edges = head_ids.shape[0]
    ends = 2 * edges
    capacity = 2 * ends // owners
    slots = owners * capacity
    own = neg_ids.shape[0]
    table = embeddings.T
    shape = jax.ShapeDtypeStruct
    groups = LANES // own
    piece = features // groups
    pay_rows = (piece + 1 + 7) // 8 * 8

    payload, place, neg_row, low_table = call(
        functools.partial(request_kernel, row_count, owners, capacity, own),
        (
            shape((owners, pay_rows, LANES), bf16),
            shape((1, ends), i32),
            shape((1, LANES), i32),
            shape((features, row_count), bf16),
        ),
        [VMEM, VMEM, SMEM, VMEM, ANY],
        [
            pltpu.VMEM((features, row_count), f32),
            pltpu.VMEM((features, LANES), f32),
            pltpu.SemaphoreType.DMA((2,)),
        ],
        limit=20 << 20,
    )(
        head_ids.reshape(1, edges),
        tail_ids.reshape(1, edges),
        neg_ids,
        slot_of.reshape(-1, LANES),
        table,
    )
    got = exchange(payload)
    answers, asked = call(
        functools.partial(answer_kernel, owners, piece),
        (shape((owners, half, LANES), bf16), shape((1, slots), i32)),
        [VMEM] * 2,
        limit=20 << 20,
    )(got, low_table)
    fetched = exchange(answers)
    neg_rows = (
        got[:, :piece, :]
        .reshape(owners, piece, groups, own)
        .transpose(0, 3, 2, 1)
        .reshape(owners * own, features)
    )
    rel_rows = call(
        relation_kernel,
        shape((features, edges), bf16),
        [VMEM] * 2,
        limit=20 << 20,
        cost=cost(2 * features * relations.shape[0] * edges, relations.size * 2),
    )(rel_ids.reshape(1, edges), relations.T)
    other_asked = lax.ppermute(asked, "rep", [(0, 1), (1, 0)])
    base = 4 * own
    outgoing = call(
        functools.partial(edge_kernel, owners),
        shape((owners, base + half, LANES), bf16),
        [VMEM] * 4,
        [pltpu.VMEM((features, slots), f32)],
        limit=30 << 20,
    )(fetched, rel_rows, neg_rows, place)
    incoming = exchange(outgoing)
    other = lax.ppermute(incoming, "rep", [(0, 1), (1, 0)])
    block = 256
    columns = lambda i: (0, i)
    fixed = lambda rank: (lambda i: (0,) * rank)
    got_specs = [
        pl.BlockSpec((owners, base + half, LANES), fixed(3)),
        pl.BlockSpec((1, slots), fixed(2)),
        pl.BlockSpec((1, LANES), fixed(2)),
    ]
    wide = pl.BlockSpec((features, block), columns)
    thin = pl.BlockSpec((1, block), columns)
    buf = pltpu.VMEM((features, slots + 2 * own), bf16)
    mine = call(
        functools.partial(sum_kernel, owners, base, own),
        shape((features, row_count), f32),
        got_specs,
        [buf],
        limit=20 << 20,
        cost=cost(2 * features * slots * row_count, 4 * features * row_count),
        grid=(row_count // block,),
        out_specs=wide,
    )(incoming, asked, neg_row)
    new_rows, new_state = call(
        functools.partial(update_kernel, owners, base, own),
        (shape((features, row_count), f32), shape((1, row_count), f32)),
        got_specs + [wide, wide, thin],
        [buf],
        limit=20 << 20,
        grid=(row_count // block,),
        out_specs=(wide, thin),
    )(other, other_asked, neg_row, mine, table, accumulator.reshape(1, row_count))
    return new_rows.T, new_state.reshape(row_count)


def split_parts(values):
    cut = values.shape[1] // 2
    return (values[:, :cut], values[:, cut:])


def edge_terms(head_rows, rel_rows, tail_rows, neg_rows):
    head_full = head_rows.astype(jnp.float32)
    rel_full = rel_rows.astype(jnp.float32)
    tail_full = tail_rows.astype(jnp.float32)
    head_re, head_im = split_parts(head_full)
    rel_re, rel_im = split_parts(rel_full)
    tail_re, tail_im = split_parts(tail_full)
    product = jnp.concatenate(
        [head_re * rel_re - head_im * rel_im, head_re * rel_im + head_im * rel_re], axis=1
    )
    product_low = product.astype(jnp.bfloat16)
    mirror_low = jnp.concatenate(
        [rel_re * tail_re + rel_im * tail_im, rel_re * tail_im - rel_im * tail_re], axis=1
    ).astype(jnp.bfloat16)
    positive = jnp.sum(product * tail_full, axis=1)
    inner_dims = (((1,), (1,)), ((), ()))
    tail_scores = lax.dot_general(
        product_low, neg_rows, inner_dims, preferred_element_type=jnp.float32
    )
    head_scores = lax.dot_general(
        mirror_low, neg_rows, inner_dims, preferred_element_type=jnp.float32
    )
    neg_count = neg_rows.shape[0]
    pos_grad = -jax.nn.sigmoid(-positive)
    tail_weight = (jax.nn.sigmoid(tail_scores) / neg_count).astype(jnp.bfloat16)
    head_weight = (jax.nn.sigmoid(head_scores) / neg_count).astype(jnp.bfloat16)
    product_grad = (
        jnp.dot(tail_weight, neg_rows, preferred_element_type=jnp.float32)
        + pos_grad[:, None] * tail_full
    )
    mirror_grad = jnp.dot(head_weight, neg_rows, preferred_element_type=jnp.float32)
    edge_dims = (((0,), (0,)), ((), ()))
    neg_grad = lax.dot_general(
        tail_weight, product_low, edge_dims, preferred_element_type=jnp.float32
    )
    neg_grad = neg_grad + lax.dot_general(
        head_weight, mirror_low, edge_dims, preferred_element_type=jnp.float32
    )
    grad_re, grad_im = split_parts(product_grad)
    head_grad = jnp.concatenate(
        [grad_re * rel_re + grad_im * rel_im, grad_im * rel_re - grad_re * rel_im], axis=1
    )
    back_re, back_im = split_parts(mirror_grad)
    tail_grad = pos_grad[:, None] * product + jnp.concatenate(
        [back_re * rel_re - back_im * rel_im, back_re * rel_im + back_im * rel_re], axis=1
    )
    return (head_grad, tail_grad, neg_grad)


def row_update(old_rows, old_state, gradient):
    new_state = old_state + jnp.mean(gradient * gradient, axis=1)
    new_rows = old_rows - step_rate * gradient / jnp.sqrt(new_state)[:, None]
    return (new_rows, new_state)


def shards(head_ids, rel_ids, tail_ids, neg_ids, slot_of, relations, embeddings, accumulator):
    row_count = embeddings.shape[0]
    feature_count = embeddings.shape[1]
    owner_count = lax.axis_size("ent")
    edge_count = head_ids.shape[0]
    end_ids = jnp.concatenate([head_ids, tail_ids])
    end_count = end_ids.shape[0]
    capacity = 2 * end_count // owner_count
    end_slots = slot_of[end_ids]
    owner_of = end_slots // row_count
    local_row = end_slots % row_count
    sorter = jnp.argsort(owner_of, stable=True)
    sorted_owner = owner_of[sorter]
    per_owner = jnp.sum(
        (owner_of[:, None] == jnp.arange(owner_count, dtype=jnp.int32)[None, :]).astype(jnp.int32),
        axis=0,
    )
    starting = jnp.cumsum(per_owner) - per_owner
    sorted_place = (
        sorted_owner * capacity + jnp.arange(end_count, dtype=jnp.int32) - starting[sorted_owner]
    )
    placed = jnp.zeros((end_count,), jnp.int32).at[sorter].set(sorted_place)
    requests = (
        jnp.full((owner_count * capacity,), -1, jnp.int32)
        .at[placed]
        .set(local_row)
        .reshape(owner_count, capacity)
    )
    low_table = embeddings.astype(jnp.bfloat16)
    asked_rows = lax.all_to_all(requests, "ent", split_axis=0, concat_axis=0, tiled=True)
    picked = jnp.where(
        (asked_rows >= 0)[:, :, None],
        low_table[jnp.maximum(asked_rows, 0)],
        jnp.zeros((), jnp.bfloat16),
    )
    returned = lax.all_to_all(picked, "ent", split_axis=0, concat_axis=0, tiled=True)
    fetched, asked_rows = (returned, asked_rows)
    end_rows = fetched.reshape(owner_count * capacity, feature_count)[placed]
    neg_local = slot_of[neg_ids] % row_count
    own_negs = low_table[neg_local]
    neg_rows = lax.all_gather(own_negs, "ent", axis=0, tiled=True)
    rel_rows = relations[rel_ids]
    head_grad, tail_grad, neg_grad = edge_terms(
        end_rows[:edge_count], rel_rows, end_rows[edge_count:], neg_rows
    )
    neg_part = lax.psum_scatter(neg_grad, "ent", scatter_dimension=0, tiled=True)
    outgoing = (
        jnp.zeros((owner_count * capacity, feature_count), jnp.float32)
        .at[placed]
        .set(jnp.concatenate([head_grad, tail_grad], axis=0))
    )
    incoming = lax.all_to_all(
        outgoing.reshape(owner_count, capacity, feature_count),
        "ent",
        split_axis=0,
        concat_axis=0,
        tiled=True,
    ).reshape(-1, feature_count)
    targets = jnp.where(asked_rows >= 0, asked_rows, row_count).reshape(-1)
    partial_sum = jax.ops.segment_sum(incoming, targets, num_segments=row_count + 1)[:row_count]
    partial_sum = partial_sum.at[neg_local].add(neg_part)
    summed = lax.psum(partial_sum, "rep")
    new_rows, new_state = row_update(embeddings, accumulator, summed)
    return (new_rows, new_state)


def fits_packed(mesh, features, rows, edges, negs, entities):
    owners = mesh.shape["ent"]
    return (
        4 * edges == owners * LANES // 2
        and mesh.shape["rep"] == 2
        and owners % 4 == 0
        and LANES % negs == 0
        and features % 16 == 0
        and features <= 4 * LANES
        and 3 * LANES < features
        and features % (LANES // negs) == 0
        and rows % 256 == 0
        and rows < 256 * 255
        and entities % LANES == 0
        and entities <= 1 << 16
    )


def any_shards(mesh, *arrays):
    head_ids, _, _, neg_ids, slot_of, _, embeddings, _ = arrays
    rows, features = embeddings.shape
    if fits_packed(mesh, features, rows, head_ids.shape[0], neg_ids.shape[0], slot_of.shape[0]):
        return packed_shards(*arrays)
    return shards(*arrays)


def solution(mesh):
    placed = (
        P(("ent", "rep")),
        P(("ent", "rep")),
        P(("ent", "rep")),
        P("ent"),
        P(),
        P(),
        P("ent", None),
        P("ent"),
    )
    return jax.shard_map(
        functools.partial(any_shards, mesh), mesh=mesh, in_specs=placed, out_specs=(P("ent", None), P("ent")), check_vma=False
    )
```

```python
import functools

import jax
import jax.numpy as jnp
from jax import lax
from jax.experimental import pallas as pl
from jax.experimental.pallas import tpu as pltpu
from jax.sharding import PartitionSpec as P

step_rate = 0.3
bf16 = jnp.bfloat16
f32 = jnp.float32
i32 = jnp.int32
LANES = 128
VMEM = pl.BlockSpec(memory_space=pltpu.VMEM)
HBM = pl.BlockSpec(memory_space=pltpu.HBM)
NN = (((1,), (0,)), ((), ()))
NT = (((1,), (1,)), ((), ()))
TN = (((0,), (0,)), ((), ()))


def mm(a, b, dims=NN):
    return lax.dot_general(a, b, dims, preferred_element_type=f32)


def iota(shape, axis):
    return lax.broadcasted_iota(i32, shape, axis)


def onehot(flags):
    return flags.astype(f32).astype(bf16)


def halves_swapped(values):
    return pltpu.roll(values, LANES // 2, 1)


def request_kernel(
    row_count, owner_count, capacity, neg_own,
    head_hbm, tail_hbm, neg_hbm, slot_hbm, emb_hbm,
    pay_ref, place_ref, neg_row_ref, table_ref,
    ids_ref, neg_ref, slot_ref, emb_buf, neg_buf, sems,
):
    edge_count = head_hbm.shape[1]
    feature_count = emb_hbm.shape[0]
    chunk = feature_count // 2
    small = [
        pltpu.make_async_copy(head_hbm, ids_ref.at[:, pl.ds(0, edge_count)], sems.at[0]),
        pltpu.make_async_copy(tail_hbm, ids_ref.at[:, pl.ds(edge_count, edge_count)], sems.at[1]),
        pltpu.make_async_copy(neg_hbm, neg_ref, sems.at[2]),
        pltpu.make_async_copy(slot_hbm, slot_ref, sems.at[3]),
    ]
    copies = [
        pltpu.make_async_copy(
            emb_hbm.at[pl.ds(c * chunk, chunk)], emb_buf.at[pl.ds(c * chunk, chunk)], sems.at[4 + c]
        )
        for c in range(2)
    ]
    for copy in small + copies:
        copy.start()
    for copy in small:
        copy.wait()
    slots = slot_ref[...]
    slots_low = (slots & 255).astype(f32).astype(bf16)
    slots_high = (slots >> 8).astype(f32).astype(bf16)

    def lookup(ids):
        count = ids.shape[1]
        picks = onehot(iota((slots.shape[0], count), 0) == (ids >> 7))
        columns = mm(slots_low, picks, TN) + 256.0 * mm(slots_high, picks, TN)
        lane_of = iota((LANES, count), 0) == (ids & 127)
        return jnp.sum(jnp.where(lane_of, columns, 0.0), axis=0, keepdims=True).astype(i32)

    ids = ids_ref[...]
    end_count = ids.shape[1]
    end_slots = lookup(ids)
    owner_of = end_slots // row_count
    local_row = end_slots - owner_of * row_count + 1
    owners = iota((owner_count, end_count), 0) == owner_of
    earlier = onehot(iota((end_count, end_count), 0) < iota((end_count, end_count), 1))
    before = mm(onehot(owners), earlier)
    rank = jnp.sum(jnp.where(owners, before, 0.0), axis=0, keepdims=True).astype(i32)
    place_ref[...] = owner_of * capacity + rank
    low = jnp.where(owners, (local_row & 255).astype(f32), 0.0).astype(bf16)
    high = jnp.where(owners, (local_row >> 8).astype(f32), 0.0).astype(bf16)
    lane = iota((LANES, end_count), 0)
    requests = mm(low, onehot(lane == rank), NT) + mm(high, onehot(lane == rank + capacity), NT)

    lane_row = iota((1, LANES), 1)
    neg_ids = jnp.zeros((1, LANES), i32)
    for n in range(neg_own):
        neg_ids = jnp.where(lane_row % neg_own == n, neg_ref[n], neg_ids)
    neg_row = lookup(neg_ids)
    neg_row = neg_row - (neg_row // row_count) * row_count
    neg_row_ref[...] = neg_row
    for copy in copies:
        copy.wait()
    table_ref[...] = emb_buf[...].astype(bf16)
    neg_buf[...] = mm(table_ref[...], onehot(iota((row_count, LANES), 0) == neg_row))
    groups = LANES // neg_own
    piece = feature_count // groups
    packed = jnp.zeros((piece, LANES), f32)
    for g in range(groups):
        packed = jnp.where(lane_row // neg_own == g, neg_buf[pl.ds(g * piece, piece), :], packed)
    neg_buf[pl.ds(0, piece), :] = packed
    neg_buf[pl.ds(piece, 8), :] = jnp.zeros((8, LANES), f32)
    whole = piece // 16 * 16
    main = neg_buf[pl.ds(0, whole), :].astype(bf16)
    rest_rows = pay_ref.shape[1] - whole
    rest = neg_buf[pl.ds(whole, rest_rows), :]
    is_request = iota((rest_rows, LANES), 0) == piece - whole
    for d in range(owner_count):
        pay_ref[d, 0:whole, :] = main
        pay_ref[d, whole : whole + rest_rows, :] = jnp.where(
            is_request, requests[d : d + 1, :], rest
        ).astype(bf16)


def pack_pair(values):
    half = values.shape[0] // 2
    real, imag = values[:half], values[half:]
    left = iota((half, LANES), 1) < LANES // 2
    first = jnp.where(left, real, halves_swapped(imag))
    second = jnp.where(left, halves_swapped(real), imag)
    return first.astype(bf16), second.astype(bf16)


def unpack_pair(first, second):
    first, second = first.astype(f32), second.astype(f32)
    left = iota(first.shape, 1) < LANES // 2
    real = jnp.where(left, first, halves_swapped(second))
    imag = jnp.where(left, halves_swapped(first), second)
    return real.astype(bf16), imag.astype(bf16)


def unpack_rows(got_ref, buf):
    half = buf.shape[0] // 2
    for s in range(0, got_ref.shape[0], 2):
        real, imag = unpack_pair(got_ref[s, 0:half, :], got_ref[s + 1, 0:half, :])
        lanes = pl.ds(s // 2 * LANES, LANES)
        buf[0:half, lanes] = real
        buf[half : 2 * half, lanes] = imag


def answer_kernel(owner_count, req_row, got_ref, table_ref, out_hbm, asked_ref, out_buf, sems):
    row_count = table_ref.shape[1]
    req = got_ref[:, req_row, :].astype(f32)
    value = req + 256.0 * halves_swapped(req)
    other = halves_swapped(value)
    left = iota((1, LANES), 1) < LANES // 2
    rows = [
        jnp.where(left, value[s : s + 1, :], other[s + 1 : s + 2, :])
        for s in range(0, owner_count, 2)
    ]
    asked = jnp.concatenate(rows, axis=1).astype(i32)
    asked_ref[...] = asked
    width = 2 * LANES
    copies = []
    for c in range(asked.shape[1] // width):
        row = asked[:, c * width : (c + 1) * width]
        picks = onehot(iota((row_count, width), 0) + 1 == row)
        rows = mm(table_ref[...], picks)
        for p in range(2):
            first, second = pack_pair(rows[:, p * LANES : (p + 1) * LANES])
            out_buf[4 * c + 2 * p] = first
            out_buf[4 * c + 2 * p + 1] = second
        part = pl.ds(4 * c, 4)
        copies.append(pltpu.make_async_copy(out_buf.at[part], out_hbm.at[part], sems.at[c]))
        copies[-1].start()
    for copy in copies:
        copy.wait()


def relation_kernel(ids_ref, relations_ref, out_ref):
    count = relations_ref.shape[1]
    picks = onehot(iota((count, ids_ref.shape[1]), 0) == ids_ref[...])
    out_ref[...] = mm(relations_ref[...], picks).astype(bf16)


def pack_neg_grad(neg_grad, out_buf, base):
    owner_count = out_buf.shape[0]
    own = neg_grad.shape[0] // owner_count
    tiles = neg_grad.shape[1] // LANES
    rest = neg_grad.shape[1] - tiles * LANES
    last = jnp.concatenate(
        [neg_grad[:, tiles * LANES :], jnp.zeros((neg_grad.shape[0], LANES - rest), f32)], axis=1
    )
    beside = pltpu.roll(last, rest, 1)
    left = iota((own // 2, LANES), 1) < rest
    for d in range(owner_count):
        first, middle, end = d * own, d * own + own // 2, (d + 1) * own
        parts = [neg_grad[first:end, t * LANES : (t + 1) * LANES] for t in range(tiles)]
        parts.append(jnp.where(left, last[first:middle], beside[middle:end]))
        packed = jnp.concatenate(parts, axis=0)
        out_buf[d, base : base + packed.shape[0], :] = packed.astype(bf16)


def neg_total(got_ref, features):
    base = features // 2
    total = got_ref[0, base:, :].astype(f32)
    for s in range(1, got_ref.shape[0]):
        total = total + got_ref[s, base:, :].astype(f32)
    tiles = features // LANES
    rest = features - tiles * LANES
    own = total.shape[0] * 2 // (2 * tiles + 1)
    last = total[tiles * own :]
    last = jnp.concatenate([last, pltpu.roll(last, LANES - rest, 1)], axis=0)[:, :rest]
    neg = jnp.concatenate([total[t * own : (t + 1) * own] for t in range(tiles)] + [last], axis=1)
    high = neg.astype(bf16)
    low = (neg - high.astype(f32)).astype(bf16)
    return jnp.concatenate([high, low], axis=0)


def edge_kernel(got_ref, rel_ref, neg_ref, place_ref, _, out_hbm, rows_buf, out_buf, sems):
    owner_count, half, _ = got_ref.shape
    slot_count = rows_buf.shape[1]
    end_count = place_ref.shape[1]
    edge_count = end_count // 2
    unpack_rows(got_ref, rows_buf)
    places = onehot(iota((slot_count, end_count), 0) == place_ref[...])
    ends = mm(rows_buf[...], places)
    head_re, head_im = ends[:half, :edge_count], ends[half:, :edge_count]
    tail_re, tail_im = ends[:half, edge_count:], ends[half:, edge_count:]
    rel = rel_ref[...].astype(f32)
    rel_re, rel_im = rel[:half], rel[half:]
    neg = neg_ref[...]
    neg_count = neg.shape[0]
    product_re = head_re * rel_re - head_im * rel_im
    product_im = head_re * rel_im + head_im * rel_re
    product_low = jnp.concatenate([product_re, product_im], axis=0).astype(bf16)
    mirror_low = jnp.concatenate(
        [rel_re * tail_re + rel_im * tail_im, rel_re * tail_im - rel_im * tail_re], axis=0
    ).astype(bf16)
    positive = jnp.sum(product_re * tail_re + product_im * tail_im, axis=0, keepdims=True)
    pos_grad = -jax.nn.sigmoid(-positive)
    tail_weight = (jax.nn.sigmoid(mm(neg, product_low)) / neg_count).astype(bf16)
    head_weight = (jax.nn.sigmoid(mm(neg, mirror_low)) / neg_count).astype(bf16)
    grad = mm(neg, tail_weight, TN)
    back = mm(neg, head_weight, TN)
    grad_re = grad[:half] + pos_grad * tail_re
    grad_im = grad[half:] + pos_grad * tail_im
    back_re, back_im = back[:half], back[half:]
    head_grad = jnp.concatenate(
        [grad_re * rel_re + grad_im * rel_im, grad_im * rel_re - grad_re * rel_im], axis=0
    ).astype(bf16)
    tail_grad = jnp.concatenate(
        [
            pos_grad * product_re + (back_re * rel_re - back_im * rel_im),
            pos_grad * product_im + (back_re * rel_im + back_im * rel_re),
        ],
        axis=0,
    ).astype(bf16)
    grads = jnp.concatenate([head_grad, tail_grad], axis=1)
    neg_grad = mm(tail_weight, product_low, NT) + mm(head_weight, mirror_low, NT)
    pack_neg_grad(neg_grad, out_buf, half)
    width = 2 * LANES
    copies = []
    for c in range(slot_count // width):
        sent = mm(grads, places[c * width : (c + 1) * width, :], NT)
        for p in range(2):
            first, second = pack_pair(sent[:, p * LANES : (p + 1) * LANES])
            out_buf[4 * c + 2 * p, 0:half, :] = first
            out_buf[4 * c + 2 * p + 1, 0:half, :] = second
        part = pl.ds(4 * c, 4)
        copies.append(pltpu.make_async_copy(out_buf.at[part], out_hbm.at[part], sems.at[c]))
        copies[-1].start()
    for copy in copies:
        copy.wait()


def target_kernel(mine_ref, other_ref, neg_row_ref, mine_out, other_out, neg_out):
    for asked_ref, out in ((mine_ref, mine_out), (other_ref, other_out)):
        slots, rows = out.shape
        down = jnp.broadcast_to(asked_ref[...], (8, slots)).T[:, 0:1]
        out[...] = onehot(iota((slots, rows), 1) + 1 == down)
    count, rows = neg_out.shape
    down = jnp.broadcast_to(neg_row_ref[...], (8, LANES)).T[:count, 0:1]
    neg_out[...] = onehot(iota((count, rows), 1) == down)


def sum_kernel(got_ref, targets_ref, neg_targets_ref, out_ref, buf):
    unpack_rows(got_ref, buf)
    neg = neg_total(got_ref, buf.shape[0])
    rows = out_ref.shape[1]
    width = 4 * LANES
    for c in range(rows // width):
        lanes = slice(c * width, (c + 1) * width)
        out_ref[:, lanes] = mm(buf[...], targets_ref[:, lanes]) + mm(
            neg, neg_targets_ref[:, lanes], TN
        )


def update_kernel(
    got_ref, targets_ref, neg_targets_ref, mine_ref, emb_ref, acc_ref,
    new_hbm, state_ref, buf, new_buf, sems,
):
    unpack_rows(got_ref, buf)
    neg = neg_total(got_ref, buf.shape[0])
    features, rows = mine_ref.shape
    width = 4 * LANES
    copies = []
    for c in range(rows // width):
        lanes = slice(c * width, (c + 1) * width)
        other = mm(buf[...], targets_ref[:, lanes]) + mm(neg, neg_targets_ref[:, lanes], TN)
        grad = mine_ref[:, lanes] + other
        state = acc_ref[:, lanes] + jnp.sum(grad * grad, axis=0, keepdims=True) / features
        state_ref[:, lanes] = state
        new_buf[:, lanes] = emb_ref[:, lanes] - grad * (step_rate / jnp.sqrt(state))
        part = pl.ds(c * width, width)
        copies.append(
            pltpu.make_async_copy(new_buf.at[:, part], new_hbm.at[:, part], sems.at[c])
        )
        copies[-1].start()
    for copy in copies:
        copy.wait()


def call(kernel, outs, in_specs, out_specs, scratch=(), limit=20 << 20, flops=0, moved=0):
    return pl.pallas_call(
        kernel,
        out_shape=outs,
        in_specs=in_specs,
        out_specs=out_specs,
        scratch_shapes=list(scratch),
        compiler_params=pltpu.CompilerParams(vmem_limit_bytes=limit),
        cost_estimate=pl.CostEstimate(flops=flops, bytes_accessed=moved, transcendentals=0),
    )


def exchange(values):
    return lax.all_to_all(values, "ent", split_axis=0, concat_axis=0, tiled=True)


def in_hbm(values):
    return pltpu.with_memory_space_constraint(values, pltpu.HBM)


def swap_cores(values):
    return lax.ppermute(values, "rep", [(0, 1), (1, 0)])


def packed_shards(
    head_ids, rel_ids, tail_ids, neg_ids, slot_of, relations, embeddings, accumulator
):
    row_count, features = embeddings.shape
    half = features // 2
    owners = lax.axis_size("ent")
    edges = head_ids.shape[0]
    ends = 2 * edges
    capacity = 2 * ends // owners
    slots = owners * capacity
    own = neg_ids.shape[0]
    table = embeddings.T
    shape = jax.ShapeDtypeStruct

    groups = LANES // own
    piece = features // groups
    pay_rows = (piece + 1 + 7) // 8 * 8
    requests, place, neg_row, low_table = call(
        functools.partial(request_kernel, row_count, owners, capacity, own),
        (
            shape((owners, pay_rows, LANES), bf16),
            shape((1, ends), i32),
            shape((1, LANES), i32),
            shape((features, row_count), bf16),
        ),
        [HBM] * 5,
        (VMEM,) * 4,
        [
            pltpu.VMEM((1, ends), i32),
            pltpu.SMEM((own,), i32),
            pltpu.VMEM((slot_of.shape[0] // LANES, LANES), i32),
            pltpu.VMEM((features, row_count), f32),
            pltpu.VMEM((features, LANES), f32),
            pltpu.SemaphoreType.DMA((6,)),
        ],
    )(
        in_hbm(head_ids.reshape(1, edges)),
        in_hbm(tail_ids.reshape(1, edges)),
        in_hbm(neg_ids),
        in_hbm(slot_of.reshape(-1, LANES)),
        in_hbm(table),
    )
    got = exchange(requests)
    sems = pltpu.SemaphoreType.DMA((slots // 256,))
    answers, asked = call(
        functools.partial(answer_kernel, owners, piece),
        (pltpu.HBM((owners, half, LANES), bf16), shape((1, slots), i32)),
        [VMEM] * 2,
        (HBM, VMEM),
        [pltpu.VMEM((owners, half, LANES), bf16), sems],
    )(got, low_table)
    fetched = exchange(answers)
    neg_rows = (
        got[:, :piece, :]
        .reshape(owners, piece, groups, own)
        .transpose(0, 3, 2, 1)
        .reshape(owners * own, features)
    )
    rel_rows = call(
        relation_kernel,
        shape((features, edges), bf16),
        [VMEM] * 2,
        VMEM,
        flops=2 * features * relations.shape[0] * edges,
        moved=relations.size * 2,
    )(rel_ids.reshape(1, edges), relations.T)
    other_asked = swap_cores(asked)
    targets, other_targets, neg_targets = call(
        target_kernel,
        (
            shape((slots, row_count), bf16),
            shape((slots, row_count), bf16),
            shape((2 * own, row_count), bf16),
        ),
        [VMEM] * 3,
        (VMEM,) * 3,
        flops=8 * slots * row_count,
        moved=4 * slots * row_count,
    )(asked, other_asked, neg_row)
    sent_rows = half + features // LANES * own + own // 2
    outgoing = call(
        edge_kernel,
        pltpu.HBM((owners, sent_rows, LANES), bf16),
        [VMEM] * 5,
        HBM,
        [pltpu.VMEM((features, slots), bf16), pltpu.VMEM((owners, sent_rows, LANES), bf16), sems],
    )(fetched, rel_rows, neg_rows, place, neg_targets)
    incoming = exchange(outgoing)
    other = swap_cores(incoming)
    buf = pltpu.VMEM((features, slots), bf16)
    mine = call(
        sum_kernel,
        shape((features, row_count), f32),
        [VMEM] * 3,
        VMEM,
        [buf],
        flops=2 * features * slots * row_count,
        moved=4 * features * row_count,
    )(incoming, targets, neg_targets)
    new_rows, new_state = call(
        update_kernel,
        (pltpu.HBM((features, row_count), f32), shape((1, row_count), f32)),
        [VMEM] * 6,
        (HBM, VMEM),
        [buf, pltpu.VMEM((features, row_count), f32), pltpu.SemaphoreType.DMA((row_count // 512,))],
    )(other, other_targets, neg_targets, mine, table, accumulator.reshape(1, row_count))
    return new_rows.T, new_state.reshape(row_count)


def split_parts(values):
    cut = values.shape[1] // 2
    return (values[:, :cut], values[:, cut:])


def edge_terms(head_rows, rel_rows, tail_rows, neg_rows):
    head_full = head_rows.astype(jnp.float32)
    rel_full = rel_rows.astype(jnp.float32)
    tail_full = tail_rows.astype(jnp.float32)
    head_re, head_im = split_parts(head_full)
    rel_re, rel_im = split_parts(rel_full)
    tail_re, tail_im = split_parts(tail_full)
    product = jnp.concatenate(
        [head_re * rel_re - head_im * rel_im, head_re * rel_im + head_im * rel_re], axis=1
    )
    product_low = product.astype(jnp.bfloat16)
    mirror_low = jnp.concatenate(
        [rel_re * tail_re + rel_im * tail_im, rel_re * tail_im - rel_im * tail_re], axis=1
    ).astype(jnp.bfloat16)
    positive = jnp.sum(product * tail_full, axis=1)
    inner_dims = (((1,), (1,)), ((), ()))
    tail_scores = lax.dot_general(
        product_low, neg_rows, inner_dims, preferred_element_type=jnp.float32
    )
    head_scores = lax.dot_general(
        mirror_low, neg_rows, inner_dims, preferred_element_type=jnp.float32
    )
    neg_count = neg_rows.shape[0]
    pos_grad = -jax.nn.sigmoid(-positive)
    tail_weight = (jax.nn.sigmoid(tail_scores) / neg_count).astype(jnp.bfloat16)
    head_weight = (jax.nn.sigmoid(head_scores) / neg_count).astype(jnp.bfloat16)
    product_grad = (
        jnp.dot(tail_weight, neg_rows, preferred_element_type=jnp.float32)
        + pos_grad[:, None] * tail_full
    )
    mirror_grad = jnp.dot(head_weight, neg_rows, preferred_element_type=jnp.float32)
    edge_dims = (((0,), (0,)), ((), ()))
    neg_grad = lax.dot_general(
        tail_weight, product_low, edge_dims, preferred_element_type=jnp.float32
    )
    neg_grad = neg_grad + lax.dot_general(
        head_weight, mirror_low, edge_dims, preferred_element_type=jnp.float32
    )
    grad_re, grad_im = split_parts(product_grad)
    head_grad = jnp.concatenate(
        [grad_re * rel_re + grad_im * rel_im, grad_im * rel_re - grad_re * rel_im], axis=1
    )
    back_re, back_im = split_parts(mirror_grad)
    tail_grad = pos_grad[:, None] * product + jnp.concatenate(
        [back_re * rel_re - back_im * rel_im, back_re * rel_im + back_im * rel_re], axis=1
    )
    return (head_grad, tail_grad, neg_grad)


def row_update(old_rows, old_state, gradient):
    new_state = old_state + jnp.mean(gradient * gradient, axis=1)
    new_rows = old_rows - step_rate * gradient / jnp.sqrt(new_state)[:, None]
    return (new_rows, new_state)


def shards(head_ids, rel_ids, tail_ids, neg_ids, slot_of, relations, embeddings, accumulator):
    row_count = embeddings.shape[0]
    feature_count = embeddings.shape[1]
    owner_count = lax.axis_size("ent")
    edge_count = head_ids.shape[0]
    end_ids = jnp.concatenate([head_ids, tail_ids])
    end_count = end_ids.shape[0]
    capacity = 2 * end_count // owner_count
    end_slots = slot_of[end_ids]
    owner_of = end_slots // row_count
    local_row = end_slots % row_count
    sorter = jnp.argsort(owner_of, stable=True)
    sorted_owner = owner_of[sorter]
    per_owner = jnp.sum(
        (owner_of[:, None] == jnp.arange(owner_count, dtype=jnp.int32)[None, :]).astype(jnp.int32),
        axis=0,
    )
    starting = jnp.cumsum(per_owner) - per_owner
    sorted_place = (
        sorted_owner * capacity + jnp.arange(end_count, dtype=jnp.int32) - starting[sorted_owner]
    )
    placed = jnp.zeros((end_count,), jnp.int32).at[sorter].set(sorted_place)
    requests = (
        jnp.full((owner_count * capacity,), -1, jnp.int32)
        .at[placed]
        .set(local_row)
        .reshape(owner_count, capacity)
    )
    low_table = embeddings.astype(jnp.bfloat16)
    asked_rows = lax.all_to_all(requests, "ent", split_axis=0, concat_axis=0, tiled=True)
    picked = jnp.where(
        (asked_rows >= 0)[:, :, None],
        low_table[jnp.maximum(asked_rows, 0)],
        jnp.zeros((), jnp.bfloat16),
    )
    returned = lax.all_to_all(picked, "ent", split_axis=0, concat_axis=0, tiled=True)
    fetched, asked_rows = (returned, asked_rows)
    end_rows = fetched.reshape(owner_count * capacity, feature_count)[placed]
    neg_local = slot_of[neg_ids] % row_count
    own_negs = low_table[neg_local]
    neg_rows = lax.all_gather(own_negs, "ent", axis=0, tiled=True)
    rel_rows = relations[rel_ids]
    head_grad, tail_grad, neg_grad = edge_terms(
        end_rows[:edge_count], rel_rows, end_rows[edge_count:], neg_rows
    )
    neg_part = lax.psum_scatter(neg_grad, "ent", scatter_dimension=0, tiled=True)
    outgoing = (
        jnp.zeros((owner_count * capacity, feature_count), jnp.float32)
        .at[placed]
        .set(jnp.concatenate([head_grad, tail_grad], axis=0))
    )
    incoming = lax.all_to_all(
        outgoing.reshape(owner_count, capacity, feature_count),
        "ent",
        split_axis=0,
        concat_axis=0,
        tiled=True,
    ).reshape(-1, feature_count)
    targets = jnp.where(asked_rows >= 0, asked_rows, row_count).reshape(-1)
    partial_sum = jax.ops.segment_sum(incoming, targets, num_segments=row_count + 1)[:row_count]
    partial_sum = partial_sum.at[neg_local].add(neg_part)
    summed = lax.psum(partial_sum, "rep")
    new_rows, new_state = row_update(embeddings, accumulator, summed)
    return (new_rows, new_state)


def fits_packed(mesh, features, rows, edges, negs, entities):
    owners = mesh.shape["ent"]
    return (
        4 * edges == owners * LANES // 2
        and mesh.shape["rep"] == 2
        and owners % 4 == 0
        and owners & (owners - 1) == 0
        and LANES % (2 * negs) == 0
        and negs == 16
        and features % (LANES // negs) == 0
        and 0 < features % LANES * 2 <= LANES
        and features % 16 == 0
        and rows % 512 == 0
        and rows < 256 * 255
        and entities % LANES == 0
        and entities <= 1 << 16
    )


def any_shards(mesh, *arrays):
    head_ids, _, _, neg_ids, slot_of, _, embeddings, _ = arrays
    rows, features = embeddings.shape
    if fits_packed(mesh, features, rows, head_ids.shape[0], neg_ids.shape[0], slot_of.shape[0]):
        return packed_shards(*arrays)
    return shards(*arrays)


def solution(mesh):
    placed = (
        P(("ent", "rep")),
        P(("ent", "rep")),
        P(("ent", "rep")),
        P("ent"),
        P(),
        P(),
        P("ent", None),
        P("ent"),
    )
    return jax.shard_map(
        functools.partial(any_shards, mesh), mesh=mesh, in_specs=placed, out_specs=(P("ent", None), P("ent")), check_vma=False
    )
```
